32 devices in a mesh: scan: 2 (over y), angle: 16 (over z, x, core).
Axes of the slice: x: 2, y: 2, z: 4, core: 2. Of those that a mesh axis runs over, the one named last changes fastest.
Arguments:
- object_init: float32 [32, 2, 128, 1024], P(('scan', 'angle')), parts along dimension 0, may hold values from -3.6 to 3.6
- measured: bfloat16 [32, 15, 128, 128], P(('scan', 'angle')), parts along dimension 0
- positions: int32 [32, 15, 2], P(('scan', 'angle')), parts along dimension 0, may hold values from 0 to 896, as said below
- angle_list: int32 [32], P('scan'), parts along dimension 0, may hold values from 0 to 15, each once
- probe: float32 [4, 128, 128], P('scan'), parts along dimension 0, may hold values from -3 to 3
- radial: float32 [16, 1024, 1024], P('angle'), may hold values from -0.1875 to 0.1875
Outputs:
- slices: float32 [32, 2, 128, 1024], P(('scan', 'angle')), parts along dimension 0
- probe_out: float32 [4, 128, 128], P('scan'), parts along dimension 0
The draws below stay inside these ranges and needn't reach their ends.
There are 2 independent parts, one for each index of `scan`. The reference program is written for one: setup_inputs(seed, part) draws one part's arguments, and reference() takes and returns one part's arrays. A program takes and returns all parts, laid end to end along the dimension named above; an argument that names none is the same for every part. Nothing has to cross between parts.
Inputs may be any that keep to these rules, and one draw needn't show every extreme that they name: `positions`: for each angle, patch number n = r * 15 + c has offsets (r * 64, c * 64) moved by at most 8 cells in each dimension and clipped so that the patch lies inside the 128 x 1024 projection.
All inputs are finite; a program needn't handle non-finite values.
Results may differ from the reference program's by a relative error of at most 0.0014.
The reference program's roundings to bfloat16 on the way count: a program that leaves them out, or rounds other values in their place, can miss the bound.
Values sent between devices are 32-bit elements; how exact they have to be, the bound alone decides.
No kernel may reach another device: no remote copies, remote signals or barrier semaphores. Data moves between devices by JAX's collectives and lax.ppermute only.
A program may use at most 64 MiB of HBM per device.

```python
import math
import jax
import jax.numpy as jnp
from jax import lax

PATCH = 128
NC = 1024
ROWS = 128
ITERS = 2
ANG = 16


def draw_positions(key, part):
    patch_rows = 2 * ROWS // PATCH - 1
    patch_cols = 2 * NC // PATCH - 1
    index = jnp.arange(patch_rows * patch_cols, dtype=jnp.int32)
    base_row = index // patch_cols * (PATCH // 2)
    base_col = index % patch_cols * (PATCH // 2)
    reach = PATCH // 16
    jitter = jax.random.randint(jax.random.fold_in(key, 11), (ANG, patch_rows * patch_cols, 2), -reach, reach + 1)
    row_at = jnp.clip(base_row[None, :] + jitter[:, :, 0], 0, ROWS - PATCH)
    col_at = jnp.clip(base_col[None, :] + jitter[:, :, 1], 0, NC - PATCH)
    return jnp.stack([row_at, col_at], -1).astype(jnp.int32)


def truth_fields(key):
    ramp = jnp.arange(ANG, dtype=jnp.float32) / max(ANG - 1, 1)
    power = 0.55 * jnp.power(3.0, ramp)
    amplitude = jnp.sqrt(power)[:, None, None, None]
    true_obj = amplitude * 0.7 * jax.random.truncated_normal(jax.random.fold_in(key, 31), -3.0, 3.0, (ANG, 2, ROWS, NC), jnp.float32)
    true_prb = 0.5 * jax.random.truncated_normal(jax.random.fold_in(key, 37), -3.0, 3.0, (2, PATCH, PATCH), jnp.float32)
    return (true_obj, true_prb)


def perturbation(key, shape, spread):
    return spread * jax.random.truncated_normal(key, -3.0, 3.0, shape, jnp.float32)


def draw_object_init(key, part):
    true_obj, true_prb = truth_fields(key)
    return true_obj + perturbation(jax.random.fold_in(key, 41), true_obj.shape, 0.3)


def draw_probe(key, part):
    true_obj, true_prb = truth_fields(key)
    return true_prb + perturbation(jax.random.fold_in(key, 43), true_prb.shape, 0.45)


def spectral_tables(count):
    index = jnp.arange(count, dtype=jnp.int32)
    phase = index[:, None] * index[None, :] % count
    angle = phase.astype(jnp.float32) * (2.0 * math.pi / count)
    scale = 1.0 / math.sqrt(count)
    return (jnp.cos(angle) * scale, jnp.sin(angle) * scale)


def draw_measured(key, part):
    true_obj, true_prb = truth_fields(key)
    offsets = draw_positions(key, part)
    cosine_theta, sine_theta = spectral_tables(PATCH)
    exact = lax.Precision.HIGHEST
    zero_index = jnp.zeros((), jnp.int32)

    def intensity(items):
        field, scan_positions = items
        pieces = jax.vmap(lambda row, col: lax.dynamic_slice(field, (zero_index, row, col), (2, PATCH, PATCH)))(scan_positions[:, 0], scan_positions[:, 1])
        piece_re, piece_im = (pieces[:, 0], pieces[:, 1])
        wave_re = true_prb[0] * piece_re - true_prb[1] * piece_im
        wave_im = true_prb[0] * piece_im + true_prb[1] * piece_re
        half_re = jnp.einsum('jk,nkl->njl', cosine_theta, wave_re, precision=exact) + jnp.einsum('jk,nkl->njl', sine_theta, wave_im, precision=exact)
        half_im = jnp.einsum('jk,nkl->njl', cosine_theta, wave_im, precision=exact) - jnp.einsum('jk,nkl->njl', sine_theta, wave_re, precision=exact)
        farfield_real = jnp.einsum('njk,kl->njl', half_re, cosine_theta, precision=exact) + jnp.einsum('njk,kl->njl', half_im, sine_theta, precision=exact)
        farfield_imaginary = jnp.einsum('njk,kl->njl', half_im, cosine_theta, precision=exact) - jnp.einsum('njk,kl->njl', half_re, sine_theta, precision=exact)
        return farfield_real * farfield_real + farfield_imaginary * farfield_imaginary
    return lax.map(intensity, (true_obj, offsets)).astype(jnp.bfloat16)


def block_scale(key, extent, cuts, least, top_value):
    factor_of, own = 1.0, jax.random.fold_in(key, 6)
    for position, shards_of in cuts:
        heights = jnp.exp(jax.random.uniform(jax.random.fold_in(own, position), (shards_of,), jnp.float32, least / len(cuts), top_value / len(cuts)))
        factor_of = factor_of * jnp.repeat(heights, extent[position] // shards_of).reshape([-1 if axis == position else 1 for axis in range(len(extent))])
    return factor_of


def normal_values(rng, dims, scale, limit, shards=(), kind=jnp.bfloat16):
    factor_of = block_scale(rng, dims, shards, -0.22, 0.18) if shards else 1.0
    drawn = jax.random.normal(rng, dims, jnp.float32) * scale * factor_of
    return jnp.minimum(jnp.maximum(drawn, -limit), limit).astype(kind)


def setup_inputs(seed: int = 0, part: int = 0) -> dict:
    streams_of = jax.random.split(jax.random.key(seed), 7)
    own_keys = jax.random.split(jax.random.fold_in(streams_of[6], part), 7)
    object_init = draw_object_init(jax.random.fold_in(jax.random.fold_in(streams_of[6], part), 71), part)
    measured = draw_measured(jax.random.fold_in(jax.random.fold_in(streams_of[6], part), 71), part)
    positions = draw_positions(jax.random.fold_in(jax.random.fold_in(streams_of[6], part), 71), part)
    angle_list = jax.random.permutation(own_keys[3], ANG).astype(jnp.int32)
    probe = draw_probe(jax.random.fold_in(jax.random.fold_in(streams_of[6], part), 71), part)
    radial = normal_values(streams_of[5], (ANG, NC, NC), NC ** -0.5, 0.1875, ((0, 16),), jnp.float32)
    return {"object_init": object_init, "measured": measured, "positions": positions, "angle_list": angle_list, "probe": probe, "radial": radial}


object_rate = 0.5
probe_rate = 1.0

def tables_exact(count, index_list):
    index = jnp.arange(count, dtype=jnp.int32)
    phase = index[:, None] * index_list[None, :] % count
    angle = phase.astype(jnp.float32) * (2.0 * math.pi / count)
    scale = 1.0 / math.sqrt(count)
    return (jnp.cos(angle) * scale, jnp.sin(angle) * scale)

def tables(count, index_list):
    cosine_part, sine_part = tables_exact(count, index_list)
    return (cosine_part.astype(jnp.bfloat16), sine_part.astype(jnp.bfloat16))

def left(table, field):
    return jnp.einsum('jk,nkl->njl', table.astype(jnp.float32), field.astype(jnp.float32))

def right(field, table):
    return jnp.einsum('njk,kl->njl', field.astype(jnp.float32), table.astype(jnp.float32))

def gradient_list(object_field, measured_intensity, scan_positions, probe_field, cosine_theta, sine_theta):
    size = probe_field.shape[1]
    zero_index = jnp.zeros((), jnp.int32)
    pieces = jax.vmap(lambda row, col: lax.dynamic_slice(object_field, (zero_index, row, col), (2, size, size)))(scan_positions[:, 0], scan_positions[:, 1])
    piece_re, piece_im = (pieces[:, 0], pieces[:, 1])
    probe_re, probe_im = (probe_field[0], probe_field[1])
    wave_re = (probe_re * piece_re - probe_im * piece_im).astype(jnp.bfloat16)
    wave_im = (probe_re * piece_im + probe_im * piece_re).astype(jnp.bfloat16)
    half_re = (left(cosine_theta, wave_re) + left(sine_theta, wave_im)).astype(jnp.bfloat16)
    half_im = (left(cosine_theta, wave_im) - left(sine_theta, wave_re)).astype(jnp.bfloat16)
    farfield_real = right(half_re, cosine_theta) + right(half_im, sine_theta)
    farfield_imaginary = right(half_im, cosine_theta) - right(half_re, sine_theta)
    residual_error = farfield_real * farfield_real + farfield_imaginary * farfield_imaginary - measured_intensity.astype(jnp.float32)
    push_re = (residual_error * farfield_real).astype(jnp.bfloat16)
    push_im = (residual_error * farfield_imaginary).astype(jnp.bfloat16)
    back_re = (left(cosine_theta, push_re) - left(sine_theta, push_im)).astype(jnp.bfloat16)
    back_im = (left(cosine_theta, push_im) + left(sine_theta, push_re)).astype(jnp.bfloat16)
    grad_re = right(back_re, cosine_theta) - right(back_im, sine_theta)
    grad_im = right(back_im, cosine_theta) + right(back_re, sine_theta)
    step_re = probe_re * grad_re + probe_im * grad_im
    step_im = probe_re * grad_im - probe_im * grad_re
    steps_all = jnp.stack([step_re, step_im], 1)

    def place(index, total):
        start = (zero_index, scan_positions[index, 0], scan_positions[index, 1])
        current = lax.dynamic_slice(total, start, (2, size, size))
        return lax.dynamic_update_slice(total, current + steps_all[index], start)
    obj_grad = lax.fori_loop(0, scan_positions.shape[0], place, jnp.zeros_like(object_field))
    pg_re = lax.optimization_barrier(jnp.sum(piece_re * grad_re + piece_im * grad_im, 0))
    pg_im = lax.optimization_barrier(jnp.sum(piece_re * grad_im - piece_im * grad_re, 0))
    energy = jnp.sum(piece_re * piece_re + piece_im * piece_im)
    return (obj_grad, jnp.stack([pg_re, pg_im], 0), energy)

def reference(object_init, measured, positions, angle_list, probe, radial):
    size = probe.shape[1]
    cosine_theta, sine_theta = tables(size, jnp.arange(size, dtype=jnp.int32))
    object_field = object_init
    probe_field = probe
    for step in range(ITERS):

        def one(items):
            return gradient_list(items[0], items[1], items[2], probe_field, cosine_theta, sine_theta)
        obj_grads, probe_grads, energies = lax.map(one, (object_field, measured, positions))
        peak = jnp.max(probe_field[0] * probe_field[0] + probe_field[1] * probe_field[1])
        object_field = object_field - object_rate / peak * obj_grads
        probe_field = probe_field - probe_rate * lax.optimization_barrier(jnp.sum(probe_grads, 0)) / (jnp.sum(energies) / (size * size))
    proj = object_field
    count = proj.shape[0]
    wave_cos, wave_sin = tables_exact(count, angle_list)
    flat = proj.reshape(count, -1)
    exact = lax.Precision.HIGHEST
    part_cos = jnp.dot(wave_cos, flat, precision=exact, preferred_element_type=jnp.float32).reshape(proj.shape)
    part_sin = jnp.dot(wave_sin, flat, precision=exact, preferred_element_type=jnp.float32).reshape(proj.shape)
    harm_re = part_cos[:, 0] + part_sin[:, 1]
    harm_im = part_cos[:, 1] - part_sin[:, 0]
    harm = jnp.stack([harm_re, harm_im], 1)

    def invert(items):
        block, matrix = items
        return jnp.dot(block.reshape(-1, block.shape[-1]), matrix, precision=exact, preferred_element_type=jnp.float32).reshape(block.shape)
    slices = lax.map(invert, (harm, radial))
    return (slices, probe_field)
```

```python
import math

import jax
import jax.numpy as jnp
import numpy as np
from jax import lax
from jax.experimental import pallas as pl
from jax.experimental.pallas import tpu as pltpu
from jax.sharding import PartitionSpec as P

ITERS = 2
LANES = 128
SUBLANES = 8

object_rate = 0.5
probe_rate = 1.0

VMEM = pl.BlockSpec(memory_space=pltpu.VMEM)
SMEM = pl.BlockSpec(memory_space=pltpu.SMEM)


def transform_tables(size):
    index = np.arange(size, dtype=np.int32)
    phase = index[:, None] * index[None, :] % size
    angle = phase.astype(np.float32) * np.float32(2.0 * math.pi / size)
    scale = np.float32(1.0 / math.sqrt(size))
    c = (np.cos(angle) * scale).astype(jnp.bfloat16)
    s = (np.sin(angle) * scale).astype(jnp.bfloat16)
    t = np.block([[c, s], [-s, c]])
    return jnp.asarray(t), jnp.asarray(np.ascontiguousarray(t.T))


def dot(a, b):
    return jnp.dot(a, b, preferred_element_type=jnp.float32)


def iterate(group, pos, obj, measured, probe, t1, t2, acc, pg, place_out):
    size = probe.shape[1]
    patches = measured.shape[0]
    tiles = obj.shape[2] // LANES
    acc[...] = jnp.zeros_like(acc)
    pg[...] = jnp.zeros_like(pg)
    lane = lax.broadcasted_iota(jnp.int32, (size, LANES), 1)
    prb_re, prb_im = probe[0], probe[1]

    def body(step, carry):
        pieces, places = [], []
        for i in range(group):
            n = step * group + i
            col = pos[n, 1]
            q = jnp.minimum(col // LANES, tiles - 2)
            rem = col - q * LANES
            low = pl.ds(pl.multiple_of(q * LANES, LANES), LANES)
            high = pl.ds(pl.multiple_of(q * LANES + LANES, LANES), LANES)
            back_shift = lax.rem(LANES - rem, LANES)
            shift = lax.rem(rem, LANES)
            mask = lane >= rem
            parts = []
            for c in range(2):
                y = jnp.where(mask, obj[c, :, low], obj[c, :, high])
                parts.append(pltpu.roll(y, back_shift, 1))
            pieces.append(parts)
            places.append((low, high, shift, mask))
        wave = jnp.concatenate(
            [
                jnp.concatenate(
                    [
                        (prb_re * a - prb_im * b).astype(jnp.bfloat16),
                        (prb_re * b + prb_im * a).astype(jnp.bfloat16),
                    ],
                    0,
                )
                for a, b in pieces
            ],
            1,
        )

        def regroup(x):
            x = x.astype(jnp.bfloat16)
            return jnp.concatenate(
                [
                    jnp.concatenate(
                        [x[:size, i * size : (i + 1) * size], x[size:, i * size : (i + 1) * size]], 1
                    )
                    for i in range(group)
                ],
                0,
            )

        half = regroup(dot(t1[...], wave))
        far = dot(half, t2[...])
        pushes = []
        for i in range(group):
            rows = slice(i * size, (i + 1) * size)
            fr, fi = far[rows, :size], far[rows, size:]
            resid = fr * fr + fi * fi - measured[step * group + i].astype(jnp.float32)
            pushes.append(
                jnp.concatenate(
                    [(resid * fr).astype(jnp.bfloat16), (resid * fi).astype(jnp.bfloat16)], 0
                )
            )
        back = regroup(dot(t2[...], jnp.concatenate(pushes, 1)))
        grad = dot(back, t1[...])
        total_re = total_im = energy = None
        for i in range(group):
            rows = slice(i * size, (i + 1) * size)
            gr, gi = grad[rows, :size], grad[rows, size:]
            a, b = pieces[i]
            re, im = a * gr + b * gi, a * gi - b * gr
            en = (a * a + b * b).reshape(size // SUBLANES, SUBLANES, LANES).sum(0)
            if total_re is None:
                total_re, total_im, energy = re, im, en
            else:
                total_re, total_im, energy = total_re + re, total_im + im, energy + en
            low, high, shift, mask = places[i]
            for c, value in ((0, prb_re * gr + prb_im * gi), (1, prb_re * gi - prb_im * gr)):
                r = pltpu.roll(value, shift, 1)
                acc[c, :, low] += jnp.where(mask, r, 0.0)
                acc[c, :, high] += jnp.where(mask, 0.0, r)
        pg[0:size] += total_re
        pg[size : 2 * size] += total_im
        pg[2 * size :] += energy
        return carry

    lax.fori_loop(0, patches // group, body, 0)
    peak = jnp.max(prb_re * prb_re + prb_im * prb_im)
    rate = object_rate / peak
    place_out(rate, acc)


GROUP = 3


def first_kernel(pos, obj, measured, probe, t1, t2, out, pg, acc):
    def finish(rate, acc):
        out[...] = obj[...] - rate * acc[...]

    iterate(GROUP, pos, obj, measured, probe, t1, t2, acc, pg, finish)


def new_probe(probe, total):
    size = probe.shape[1]
    energy = jnp.sum(total[2 * size :]) / (size * size)
    return probe[...] - probe_rate * total[: 2 * size].reshape(probe.shape) / energy


def second_kernel(pos, obj, measured, probe, total, t1, t2, out, prb_out, pg, acc):
    prb_out[...] = new_probe(probe, total)

    def finish(rate, acc):
        value = obj[...] - rate * acc[...]
        tiles = value.shape[2] // LANES
        for r in range(value.shape[1] // SUBLANES):
            for t in range(tiles):
                for c in range(2):
                    out[r * tiles + t, c] = value[c, r * 8 : r * 8 + 8, t * 128 : t * 128 + 128]

    iterate(GROUP, pos, obj, measured, prb_out, t1, t2, acc, pg, finish)


def butterfly(values):
    n = len(values)
    if n == 1:
        return values
    even, odd = butterfly(values[::2]), butterfly(values[1::2])
    low, high = [], []
    for k in range(n // 2):
        (er, ei), (xr, xi) = even[k], odd[k]
        c, s = math.cos(2 * math.pi * k / n), -math.sin(2 * math.pi * k / n)
        if k == 0:
            tr, ti = xr, xi
        elif 4 * k == n:
            tr, ti = xi, -xr
        elif 8 * k == n:
            tr, ti = (xr + xi) * c, (xi - xr) * c
        elif 8 * k == 3 * n:
            tr, ti = (xr * c - xi * s), (xr * s + xi * c)
        else:
            tr, ti = xr * c - xi * s, xr * s + xi * c
        low.append((er + tr, ei + ti))
        high.append((er - tr, ei - ti))
    return low + high


def angular_kernel(angles, blocks, out, where):
    count = blocks.shape[0]

    def note(b, carry):
        where[angles[b]] = b
        return carry

    lax.fori_loop(0, count, note, 0)
    scale = 1.0 / math.sqrt(count)

    def cell(j, carry):
        values = []
        for a in range(count):
            block = blocks[where[a], j]
            values.append((block[0] * scale, block[1] * scale))
        for k, (re, im) in enumerate(butterfly(values)):
            out[k, j, 0] = re
            out[k, j, 1] = im
        return carry

    lax.fori_loop(0, blocks.shape[1], cell, 0)


def split(x):
    high = x.astype(jnp.bfloat16)
    return high, (x - high.astype(jnp.float32)).astype(jnp.bfloat16)


def prepare_kernel(radial, high, low):
    high[...], low[...] = split(radial[...])


def invert_kernel(harm, r_high, r_low, out, x_high, x_low):
    cells, _, rows, lanes = harm.shape
    tiles = r_high.shape[0] // lanes
    height = cells // tiles * rows
    for r in range(cells // tiles):
        for t in range(tiles):
            for c in range(2):
                high, low = split(harm[r * tiles + t, c])
                x_high[c * height + r * 8 : c * height + r * 8 + 8, t * 128 : t * 128 + 128] = high
                x_low[c * height + r * 8 : c * height + r * 8 + 8, t * 128 : t * 128 + 128] = low
    value = dot(x_high[...], r_high[...]) + (
        dot(x_high[...], r_low[...]) + dot(x_low[...], r_high[...])
    )
    out[...] = value.reshape(out.shape)


def call(kernel, out_shape, args, scratch=(), flops=0, specs=None):
    moved = sum(math.prod(x.shape) * x.dtype.itemsize for x in (*args, *jax.tree.leaves(out_shape)))
    return pl.pallas_call(
        kernel,
        out_shape=out_shape,
        in_specs=specs or [VMEM] * len(args),
        out_specs=jax.tree.map(lambda _: VMEM, out_shape),
        scratch_shapes=scratch,
        cost_estimate=pl.CostEstimate(flops=flops, bytes_accessed=moved, transcendentals=0),
        name=kernel.__name__,
    )(*args)


def all_sum(message, size, energy_rows, axis, count):
    inner = 1 << ((count.bit_length() - 1 + 1) // 2)
    outer = count // inner
    me = lax.axis_index(axis)
    low = me % inner

    def swap(x, mask):
        return lax.ppermute(x, axis, [(i, i ^ mask) for i in range(count)])

    part = size // inner
    body = message[:size].reshape(inner, part, LANES)
    tail = message[size:]
    chunks = [
        jnp.concatenate([lax.dynamic_index_in_dim(body, low ^ m, 0, False), tail], 0) for m in range(inner)
    ]
    total = chunks[0]
    for x in [swap(chunks[m], m) for m in range(1, inner)]:
        total = total + x
    parts = [swap(total, m * inner) for m in range(1, outer)]
    for x in parts:
        total = total + x
    mine, tail = total[:part], total[part:]
    parts = [mine] + [swap(mine, m) for m in range(1, inner)]
    whole = jnp.zeros((inner, part, LANES), message.dtype)
    for m in range(inner):
        whole = lax.dynamic_update_index_in_dim(whole, parts[m], low ^ m, 0)
    return jnp.concatenate([whole.reshape(size, LANES), tail], 0)


def on_device(count, object_init, measured, positions, angle_list, probe, radial):
    f32, bf16 = jnp.float32, jnp.bfloat16
    shape = jax.ShapeDtypeStruct
    size = probe.shape[1]
    rows, columns = object_init.shape[2:]
    cells = rows // SUBLANES * (columns // LANES)
    patches = measured.shape[1]
    assert object_init.shape[0] == 1 and rows == size == LANES and cells % count == 0
    t1, t2 = transform_tables(size)
    obj, meas, pos = object_init[0], measured[0], positions[0]
    flops = patches * 4 * 2 * (2 * size) * (2 * size) * size
    message = shape((2 * size + SUBLANES, LANES), f32)
    obj, part = call(
        first_kernel,
        (shape(obj.shape, f32), message),
        (pos, obj, meas, probe, t1, t2),
        [pltpu.VMEM(obj.shape, f32)],
        flops,
        [SMEM] + [VMEM] * 5,
    )
    r_high, r_low = call(
        prepare_kernel, (shape(radial.shape[1:], bf16),) * 2, (radial[0],), flops=3 * radial.size
    )
    total = all_sum(part, 2 * size, SUBLANES, "angle", count)
    blocks, prb, part = call(
        second_kernel,
        (shape((cells, 2, SUBLANES, LANES), f32), shape(probe.shape, f32), message),
        (pos, obj, meas, probe, total, t1, t2),
        [pltpu.VMEM(obj.shape, f32)],
        flops,
        [SMEM] + [VMEM] * 6,
    )
    blocks = lax.all_to_all(blocks, "angle", split_axis=0, concat_axis=0, tiled=True)
    harm = call(
        angular_kernel,
        shape((count, cells // count, 2, SUBLANES, LANES), f32),
        (angle_list, blocks.reshape(count, cells // count, 2, SUBLANES, LANES)),
        [pltpu.SMEM((count,), jnp.int32)],
        10 * blocks.size,
        [SMEM, VMEM],
    ).reshape(blocks.shape)
    harm = lax.all_to_all(harm, "angle", split_axis=0, concat_axis=0, tiled=True)
    slices = call(
        invert_kernel,
        shape(object_init.shape[1:], f32),
        (harm, r_high, r_low),
        [pltpu.VMEM((2 * rows, columns), bf16)] * 2,
        6 * 2 * rows * columns * columns,
    )
    total = all_sum(part, 2 * size, SUBLANES, "angle", count)
    energy = jnp.sum(total[2 * size :]) / (size * size)
    probe_out = prb - probe_rate * total[: 2 * size].reshape(prb.shape) / energy
    return slices[None], probe_out


def solution(mesh):
    count = mesh.shape["angle"]

    def body(*args):
        return on_device(count, *args)

    in_specs = (
        P(("scan", "angle"), None, None, None),
        P(("scan", "angle"), None, None, None),
        P(("scan", "angle"), None, None),
        P("scan"),
        P("scan", None, None),
        P("angle", None, None),
    )
    out_specs = (P(("scan", "angle"), None, None, None), P("scan", None, None))
    return jax.shard_map(body, mesh=mesh, in_specs=in_specs, out_specs=out_specs, check_vma=False)
```

```python
import functools
import math

import jax
import jax.numpy as jnp
import numpy as np
from jax import lax
from jax.experimental import pallas as pl
from jax.experimental.pallas import tpu as pltpu
from jax.sharding import PartitionSpec as P


LANES = 128
SUBLANES = 8

object_rate = 0.5
probe_rate = 1.0

VMEM = pl.BlockSpec(memory_space=pltpu.VMEM)
SMEM = pl.BlockSpec(memory_space=pltpu.SMEM)


def transform_tables(size):
    index = np.arange(size, dtype=np.int32)
    phase = index[:, None] * index[None, :] % size
    angle = phase.astype(np.float32) * np.float32(2.0 * math.pi / size)
    scale = np.float32(1.0 / math.sqrt(size))
    c = (np.cos(angle) * scale).astype(jnp.bfloat16)
    s = (np.sin(angle) * scale).astype(jnp.bfloat16)
    t = np.block([[c, s], [-s, c]])
    return jnp.asarray(t), jnp.asarray(np.ascontiguousarray(t.T))


def dot(a, b):
    return jnp.dot(a, b, preferred_element_type=jnp.float32)


def window(pos, n, tiles):
    col = pos[1, n]
    q = jnp.minimum(col // LANES, tiles - 2)
    rem = col - q * LANES
    return q, rem


def cut(load, q, rem, mask):
    y = jnp.where(mask, load(q), load(q + 1))
    return pltpu.roll(y, lax.rem(LANES - rem, LANES), 1)


def iterate(pos, piece, measured, probe, t1, t2, out, pg):
    size = probe.shape[1]
    patches = measured.shape[0]
    tiles = out.shape[0] // (size // SUBLANES)
    view = out.reshape(size // SUBLANES, tiles, 2, SUBLANES, LANES)
    lane = lax.broadcasted_iota(jnp.int32, (size, LANES), 1)
    prb_re, prb_im = probe[0], probe[1]
    rate = object_rate / jnp.max(prb_re * prb_re + prb_im * prb_im)

    def both(a, b):
        return jnp.concatenate([a.astype(jnp.bfloat16), b.astype(jnp.bfloat16)], 0)

    def regroup(x):
        x = x.astype(jnp.bfloat16)
        spans = [slice(i * size, (i + 1) * size) for i in range(patches)]
        return jnp.concatenate([jnp.concatenate([x[:size, p], x[size:, p]], 1) for p in spans], 0)

    waves = []
    for n in range(patches):
        a, b = piece(n)
        waves.append(both(prb_re * a - prb_im * b, prb_re * b + prb_im * a))
    half = regroup(dot(t1[...], jnp.concatenate(waves, 1)))
    far = dot(half, t2[...])
    pushes = []
    for n in range(patches):
        rows = slice(n * size, (n + 1) * size)
        fr, fi = far[rows, :size], far[rows, size:]
        resid = fr * fr + fi * fi - measured[n].astype(jnp.float32)
        pushes.append(both(resid * fr, resid * fi))
    back = regroup(dot(t2[...], jnp.concatenate(pushes, 1)))
    grad = dot(back, t1[...])
    total_re = total_im = 0.0
    step_re, step_im = prb_re * rate, prb_im * rate
    for n in range(patches):
        rows = slice(n * size, (n + 1) * size)
        gr, gi = grad[rows, :size], grad[rows, size:]
        a, b = piece(n)
        total_re, total_im = total_re + (a * gr + b * gi), total_im + (a * gi - b * gr)
        q, rem = window(pos, n, tiles)
        mask = lane >= rem
        for c, value in ((0, step_re * gr + step_im * gi), (1, step_re * gi - step_im * gr)):
            r = pltpu.roll(value, lax.rem(rem, LANES), 1)
            for t, part in ((q, jnp.where(mask, r, 0.0)), (q + 1, jnp.where(mask, 0.0, r))):
                view[:, t, c] = view[:, t, c] - part.reshape(size // SUBLANES, SUBLANES, LANES)
    pg[:size] = total_re
    pg[size : 2 * size] = total_im


def energy_of(piece, patches):
    total = 0.0
    for n in range(patches):
        for x in piece(n):
            total = total + (x * x).reshape(-1, SUBLANES, LANES).sum(0)
    return total


def hand_out(low, pg, parts):
    height = parts[0].shape[0] - SUBLANES
    for m, part in enumerate(parts):
        start = pl.multiple_of((low[0] ^ m) * height, SUBLANES)
        part[:height] = pg[pl.ds(start, height)]
        part[height:] = pg[height * len(parts) :]


def collect(low, blocks, probe, out):
    height = blocks[0].shape[0] - SUBLANES
    size = probe.shape[1]
    energy = jnp.sum(blocks[0][height:]) / (size * size)
    share = min(height, size)
    for m, block in enumerate(blocks):
        for piece in range(height // share):
            start = (low[0] ^ m) * height + piece * share
            where = (start // size, pl.ds(pl.multiple_of(start % size, SUBLANES), share))
            gradient = block[piece * share : piece * share + share]
            out[where] = probe[where] - probe_rate * gradient / energy


def first_kernel(inner, low, pos, obj_far, measured_far, probe_far, t1_far, t2_far, out, *refs):
    parts, (obj, measured, probe, t1, t2, pieces, pg, sem) = refs[:inner], refs[inner:]
    pairs = ((probe_far, probe), (obj_far, obj), (t1_far, t1), (t2_far, t2), (measured_far, measured))
    copies = [pltpu.make_async_copy(far, near, sem.at[i]) for i, (far, near) in enumerate(pairs)]
    for copy in copies:
        copy.start()
    size = probe.shape[1]
    patches, tiles = measured.shape[0], obj.shape[2] // LANES
    lane = lax.broadcasted_iota(jnp.int32, (size, LANES), 1)
    copies[0].wait()
    copies[1].wait()
    for n in range(patches):
        q, rem = window(pos, n, tiles)
        mask = lane >= rem
        for c in range(2):

            def load(t):
                return obj[c, :, pl.ds(pl.multiple_of(t * LANES, LANES), LANES)]

            pieces[n, c] = cut(load, q, rem, mask)
    for r in range(size // SUBLANES):
        for t in range(tiles):
            for c in range(2):
                out[r * tiles + t, c] = obj[c, r * 8 : r * 8 + 8, t * 128 : t * 128 + 128]

    def piece(n):
        return pieces[n, 0], pieces[n, 1]

    pg[2 * size :] = energy_of(piece, patches)
    for copy in copies[2:]:
        copy.wait()
    iterate(pos, piece, measured, probe, t1, t2, out, pg)
    hand_out(low, pg, parts)


def cut_kernel(pos, obj, pieces, energy):
    patches, _, size, _ = pieces.shape
    tiles = obj.shape[0] // (size // SUBLANES)
    view = obj.reshape(size // SUBLANES, tiles, 2, SUBLANES, LANES)
    lane = lax.broadcasted_iota(jnp.int32, (size, LANES), 1)
    energy[...] = jnp.zeros_like(energy)

    def body(n, carry):
        q, rem = window(pos, n, tiles)
        mask = lane >= rem
        for c in range(2):
            x = cut(lambda t: view[:, t, c].reshape(size, LANES), q, rem, mask)
            pieces[n, c] = x
            energy[...] += (x * x).reshape(-1, SUBLANES, LANES).sum(0)
        return carry

    lax.fori_loop(0, patches, body, 0)


def second_kernel(inner, low, pos, obj, pieces, energy, measured, probe, t1, t2, *refs):
    blocks, (prb_out, out), parts, pg = refs[:inner], refs[inner : inner + 2], refs[inner + 2 : -1], refs[-1]
    size = probe.shape[1]
    collect(low, blocks, probe, prb_out)
    pg[2 * size :] = energy[...]
    out[...] = obj[...]
    iterate(pos, lambda n: (pieces[n, 0], pieces[n, 1]), measured, prb_out, t1, t2, out, pg)
    hand_out(low, pg, parts)


def probe_kernel(low, probe, *refs):
    collect(low, refs[:-1], probe, refs[-1])


def butterfly(values):
    n = len(values)
    if n == 1:
        return values
    even, odd = butterfly(values[::2]), butterfly(values[1::2])
    low, high = [], []
    for k in range(n // 2):
        (er, ei), (xr, xi) = even[k], odd[k]
        c, s = math.cos(2 * math.pi * k / n), -math.sin(2 * math.pi * k / n)
        if k == 0:
            tr, ti = xr, xi
        elif 4 * k == n:
            tr, ti = xi, -xr
        elif 8 * k == n:
            tr, ti = (xr + xi) * c, (xi - xr) * c
        elif 8 * k == 3 * n:
            tr, ti = (xr * c - xi * s), (xr * s + xi * c)
        else:
            tr, ti = xr * c - xi * s, xr * s + xi * c
        low.append((er + tr, ei + ti))
        high.append((er - tr, ei - ti))
    return low + high


def angular_kernel(angles, blocks, out, where):
    count = blocks.shape[0]

    def note(b, carry):
        where[angles[b]] = b
        return carry

    lax.fori_loop(0, count, note, 0)
    scale = 1.0 / math.sqrt(count)

    def cell(j, carry):
        values = []
        for a in range(count):
            block = blocks[where[a], j]
            values.append((block[0] * scale, block[1] * scale))
        for k, (re, im) in enumerate(butterfly(values)):
            out[k, j, 0] = re
            out[k, j, 1] = im
        return carry

    lax.fori_loop(0, blocks.shape[1], cell, 0)


def split(x):
    high = x.astype(jnp.bfloat16)
    return high, (x - high.astype(jnp.float32)).astype(jnp.bfloat16)


def prepare_kernel(radial, high, low):
    high[...], low[...] = split(radial[...])


def invert_kernel(harm, r_high, r_low_far, out, x_high, x_low, r_low, sem):
    copy = pltpu.make_async_copy(r_low_far, r_low, sem)
    copy.start()
    cells, _, rows, lanes = harm.shape
    tiles = r_high.shape[0] // lanes
    height = cells // tiles * rows
    for r in range(cells // tiles):
        for t in range(tiles):
            for c in range(2):
                where = (slice(c * height + r * 8, c * height + r * 8 + 8), slice(t * 128, t * 128 + 128))
                x_high[where], x_low[where] = split(harm[r * tiles + t, c])
    value = dot(x_high[...], r_high[...]) + dot(x_low[...], r_high[...])
    copy.wait()
    out[...] = (value + dot(x_high[...], r_low[...])).reshape(out.shape)


HBM = pltpu.MemorySpace.HBM


def call(kernel, out_shape, args, scratch=(), flops=0, scalars=0, far=(), limit=2):
    moved = sum(math.prod(x.shape) * x.dtype.itemsize for x in (*args, *jax.tree.leaves(out_shape)))
    specs = [SMEM] * scalars + [VMEM] * (len(args) - scalars)
    args = list(args)
    for i in far:
        args[i] = pltpu.with_memory_space_constraint(args[i], HBM)
        if i >= scalars:
            specs[i] = pl.BlockSpec(memory_space=HBM)
    return pl.pallas_call(
        kernel,
        out_shape=out_shape,
        in_specs=specs,
        out_specs=jax.tree.map(lambda _: VMEM, out_shape),
        scratch_shapes=scratch,
        cost_estimate=pl.CostEstimate(flops=flops, bytes_accessed=moved, transcendentals=0),
        compiler_params=pltpu.CompilerParams(vmem_limit_bytes=limit << 20),
    )(*args)


def merge_kernel(*refs):
    total = refs[0][...]
    for x in refs[1:-1]:
        total = total + x[...]
    refs[-1][...] = total


def merge(parts):
    return call(merge_kernel, jax.ShapeDtypeStruct(parts[0].shape, parts[0].dtype), parts)


def all_sum(parts, axis, count):
    inner = len(parts)
    outer = count // inner

    def swap(x, mask):
        return lax.ppermute(x, axis, [(i, i ^ mask) for i in range(count)])

    others = [swap(parts[m], m) for m in range(1, inner)]
    total = merge([parts[0], *others])
    others = [swap(total, m * inner) for m in range(1, outer)]
    total = merge([total, *others])
    return [total] + [swap(total, m) for m in range(1, inner)]


def on_device(count, object_init, measured, positions, angle_list, probe, radial):
    f32, bf16 = jnp.float32, jnp.bfloat16
    shape = jax.ShapeDtypeStruct
    size = probe.shape[1]
    rows, columns = object_init.shape[2:]
    cells = rows // SUBLANES * (columns // LANES)
    patches = measured.shape[1]
    assert object_init.shape[0] == 1 and rows == size == LANES and cells % count == 0
    t1, t2 = transform_tables(size)
    obj, meas, pos = object_init[0], measured[0], positions[0].T
    flops = patches * 4 * 2 * (2 * size) * (2 * size) * size
    inner = 1 << (count.bit_length() // 2)
    low = (lax.axis_index("angle") & (inner - 1)).reshape(1)
    messages = [shape((2 * size // inner + SUBLANES, LANES), f32)] * inner
    field = shape((cells, 2, SUBLANES, LANES), f32)
    windows = (patches, 2, size, LANES)
    gradient = pltpu.VMEM((2 * size + SUBLANES, LANES), f32)
    obj, *parts = call(
        functools.partial(first_kernel, inner),
        [field, *messages],
        (low, pos, obj, meas, probe, t1, t2),
        [pltpu.VMEM(x.shape, x.dtype) for x in (obj, meas, probe, t1, t2)]
        + [pltpu.VMEM(windows, f32), gradient, pltpu.SemaphoreType.DMA((5,))],
        flops,
        2,
        far=range(1, 7),
        limit=16,
    )
    pieces, energy = call(
        cut_kernel, [shape(windows, f32), shape((SUBLANES, LANES), f32)], (pos, obj), (), 10 * obj.size, 1
    )
    r_high, r_low = call(prepare_kernel, [shape(radial.shape[1:], bf16)] * 2, (radial[0],), flops=3 * radial.size)
    blocks = all_sum(parts, "angle", count)
    prb, obj, *parts = call(
        functools.partial(second_kernel, inner),
        [shape(probe.shape, f32), field, *messages],
        (low, pos, obj, pieces, energy, meas, probe, t1, t2, *blocks),
        [gradient],
        flops,
        2,
        limit=16,
    )

    def exchange(x):
        return lax.all_to_all(x, "angle", split_axis=0, concat_axis=0, tiled=True)

    received = exchange(obj)
    grouped = shape((count, cells // count, 2, SUBLANES, LANES), f32)
    harm = call(
        angular_kernel,
        grouped,
        (angle_list, received.reshape(grouped.shape)),
        [pltpu.SMEM((count,), jnp.int32)],
        10 * received.size,
        1,
        limit=8,
    ).reshape(field.shape)
    harm = exchange(harm)
    slices = call(
        invert_kernel,
        shape(object_init.shape[1:], f32),
        (harm, r_high, r_low),
        [pltpu.VMEM((2 * rows, columns), bf16)] * 2
        + [pltpu.VMEM(r_low.shape, bf16), pltpu.SemaphoreType.DMA],
        6 * 2 * rows * columns * columns,
        0,
        far=(2,),
        limit=12,
    )
    blocks = all_sum(parts, "angle", count)
    probe_out = call(probe_kernel, shape(probe.shape, f32), (low, prb, *blocks), scalars=1)
    return slices[None], probe_out


def solution(mesh):
    count = mesh.shape["angle"]

    def body(*args):
        return on_device(count, *args)

    in_specs = (
        P(("scan", "angle"), None, None, None),
        P(("scan", "angle"), None, None, None),
        P(("scan", "angle"), None, None),
        P("scan"),
        P("scan", None, None),
        P("angle", None, None),
    )
    out_specs = (P(("scan", "angle"), None, None, None), P("scan", None, None))
    return jax.shard_map(body, mesh=mesh, in_specs=in_specs, out_specs=out_specs, check_vma=False)
```

```python
import functools
import math

import jax
import jax.numpy as jnp
import numpy as np
from jax import lax
from jax.experimental import pallas as pl
from jax.experimental.pallas import tpu as pltpu
from jax.sharding import PartitionSpec as P


LANES = 128
SUBLANES = 8

object_rate = 0.5
probe_rate = 1.0

VMEM = pl.BlockSpec(memory_space=pltpu.VMEM)
SMEM = pl.BlockSpec(memory_space=pltpu.SMEM)


def transform_tables(size):
    index = np.arange(size, dtype=np.int32)
    phase = index[:, None] * index[None, :] % size
    angle = phase.astype(np.float32) * np.float32(2.0 * math.pi / size)
    scale = np.float32(1.0 / math.sqrt(size))
    c = (np.cos(angle) * scale).astype(jnp.bfloat16)
    s = (np.sin(angle) * scale).astype(jnp.bfloat16)
    t = np.block([[c, s], [-s, c]])
    return jnp.asarray(t), jnp.asarray(np.ascontiguousarray(t.T))


def dot(a, b):
    return jnp.dot(a, b, preferred_element_type=jnp.float32)


def window(pos, n, tiles):
    col = pos[1, n]
    q = jnp.minimum(col // LANES, tiles - 2)
    rem = col - q * LANES
    return q, rem


def cut(load, q, rem, mask):
    y = jnp.where(mask, load(q), load(q + 1))
    return pltpu.roll(y, lax.rem(LANES - rem, LANES), 1)


def iterate(pos, piece, measured, probe, t1, t2, out, pg):
    size = probe.shape[1]
    patches = measured.shape[0]
    tiles = out.shape[0] // (size // SUBLANES)
    view = out.reshape(size // SUBLANES, tiles, 2, SUBLANES, LANES)
    lane = lax.broadcasted_iota(jnp.int32, (size, LANES), 1)
    prb_re, prb_im = probe[0], probe[1]
    rate = object_rate / jnp.max(prb_re * prb_re + prb_im * prb_im)

    def both(a, b):
        return jnp.concatenate([a.astype(jnp.bfloat16), b.astype(jnp.bfloat16)], 0)

    def regroup(x):
        x = x.astype(jnp.bfloat16)
        spans = [slice(i * size, (i + 1) * size) for i in range(patches)]
        return jnp.concatenate([jnp.concatenate([x[:size, p], x[size:, p]], 1) for p in spans], 0)

    waves = []
    for n in range(patches):
        a, b = piece(n)
        waves.append(both(prb_re * a - prb_im * b, prb_re * b + prb_im * a))
    half = regroup(dot(t1[...], jnp.concatenate(waves, 1)))
    far = dot(half, t2[...])
    pushes = []
    for n in range(patches):
        rows = slice(n * size, (n + 1) * size)
        fr, fi = far[rows, :size], far[rows, size:]
        resid = fr * fr + fi * fi - measured[n].astype(jnp.float32)
        pushes.append(both(resid * fr, resid * fi))
    back = regroup(dot(t2[...], jnp.concatenate(pushes, 1)))
    grad = dot(back, t1[...])
    total_re = total_im = 0.0
    step_re, step_im = prb_re * rate, prb_im * rate
    for n in range(patches):
        rows = slice(n * size, (n + 1) * size)
        gr, gi = grad[rows, :size], grad[rows, size:]
        a, b = piece(n)
        total_re, total_im = total_re + (a * gr + b * gi), total_im + (a * gi - b * gr)
        q, rem = window(pos, n, tiles)
        mask = lane >= rem
        for c, value in ((0, step_re * gr + step_im * gi), (1, step_re * gi - step_im * gr)):
            r = pltpu.roll(value, lax.rem(rem, LANES), 1)
            r = r.reshape(size // SUBLANES, SUBLANES, LANES)
            for t, own in ((q, mask), (q + 1, ~mask)):
                pltpu.store(view.at[:, t, c], view[:, t, c] - r, mask=own.reshape(r.shape))
    pg[:size] = total_re
    pg[size : 2 * size] = total_im


def energy_of(piece, patches):
    total = 0.0
    for n in range(patches):
        for x in piece(n):
            total = total + (x * x).reshape(-1, SUBLANES, LANES).sum(0)
    return total


def hand_out(low, pg, parts):
    height = parts[0].shape[0] - SUBLANES
    for m, part in enumerate(parts):
        start = pl.multiple_of((low[0] & (len(parts) - 1) ^ m) * height, SUBLANES)
        part[:height] = pg[pl.ds(start, height)]
        part[height:] = pg[height * len(parts) :]


def collect(low, blocks, probe, out):
    height = blocks[0].shape[0] - SUBLANES
    size = probe.shape[1]
    energy = jnp.sum(blocks[0][height:]) / (size * size)
    share = min(height, size)
    for m, block in enumerate(blocks):
        for piece in range(height // share):
            start = (low[0] & (len(blocks) - 1) ^ m) * height + piece * share
            where = (start // size, pl.ds(pl.multiple_of(start % size, SUBLANES), share))
            gradient = block[piece * share : piece * share + share]
            out[where] = probe[where] - probe_rate * gradient / energy


def first_kernel(inner, low, pos, obj_far, measured_far, probe_far, t1_far, t2_far, out, *refs):
    parts, (obj, measured, probe, t1, t2, pieces, pg, sem) = refs[:inner], refs[inner:]
    pairs = ((probe_far, probe), (obj_far, obj), (t1_far, t1), (t2_far, t2), (measured_far, measured))
    copies = [pltpu.make_async_copy(far, near, sem.at[i]) for i, (far, near) in enumerate(pairs)]
    for copy in copies:
        copy.start()
    size = probe.shape[1]
    patches, tiles = measured.shape[0], obj.shape[2] // LANES
    lane = lax.broadcasted_iota(jnp.int32, (size, LANES), 1)
    copies[0].wait()
    copies[1].wait()
    for n in range(patches):
        q, rem = window(pos, n, tiles)
        mask = lane >= rem
        for c in range(2):

            def load(t):
                return obj[c, :, pl.ds(pl.multiple_of(t * LANES, LANES), LANES)]

            pieces[n, c] = cut(load, q, rem, mask)
    for r in range(size // SUBLANES):
        for t in range(tiles):
            for c in range(2):
                out[r * tiles + t, c] = obj[c, r * 8 : r * 8 + 8, t * 128 : t * 128 + 128]

    def piece(n):
        return pieces[n, 0], pieces[n, 1]

    pg[2 * size :] = energy_of(piece, patches)
    for copy in copies[2:]:
        copy.wait()
    iterate(pos, piece, measured, probe, t1, t2, out, pg)
    hand_out(low, pg, parts)


def cut_kernel(pos, obj, pieces, energy):
    patches, _, size, _ = pieces.shape
    tiles = obj.shape[0] // (size // SUBLANES)
    view = obj.reshape(size // SUBLANES, tiles, 2, SUBLANES, LANES)
    lane = lax.broadcasted_iota(jnp.int32, (size, LANES), 1)
    energy[...] = jnp.zeros_like(energy)

    def body(n, carry):
        q, rem = window(pos, n, tiles)
        mask = lane >= rem
        for c in range(2):
            x = cut(lambda t: view[:, t, c].reshape(size, LANES), q, rem, mask)
            pieces[n, c] = x
            energy[...] += (x * x).reshape(-1, SUBLANES, LANES).sum(0)
        return carry

    lax.fori_loop(0, patches, body, 0)


def second_kernel(inner, low, pos, obj, pieces, energy, measured, probe, t1, t2, *refs):
    blocks, prb_out, out, parts, pg = refs[:inner], refs[inner], refs[inner + 1], refs[inner + 2 : -1], refs[-1]
    size = probe.shape[1]
    collect(low, blocks, probe, prb_out)
    pg[2 * size :] = energy[...]
    out[...] = obj[...]
    iterate(pos, lambda n: (pieces[n, 0], pieces[n, 1]), measured, prb_out, t1, t2, out, pg)
    hand_out(low, pg, parts)


def probe_kernel(low, probe, *refs):
    collect(low, refs[:-1], probe, refs[-1])


def butterfly(values):
    n = len(values)
    if n == 1:
        return values
    even, odd = butterfly(values[::2]), butterfly(values[1::2])
    low, high = [], []
    for k in range(n // 2):
        (er, ei), (xr, xi) = even[k], odd[k]
        c, s = math.cos(2 * math.pi * k / n), -math.sin(2 * math.pi * k / n)
        if k == 0:
            tr, ti = xr, xi
        elif 4 * k == n:
            tr, ti = xi, -xr
        elif 8 * k == n:
            tr, ti = (xr + xi) * c, (xi - xr) * c
        elif 8 * k == 3 * n:
            tr, ti = (xr * c - xi * s), (xr * s + xi * c)
        else:
            tr, ti = xr * c - xi * s, xr * s + xi * c
        low.append((er + tr, ei + ti))
        high.append((er - tr, ei - ti))
    return low + high


def angular_kernel(angles, blocks, far, where, out, sem):
    count, share = blocks.shape[:2]

    def note(b, carry):
        where[angles[b]] = b
        return carry

    lax.fori_loop(0, count, note, 0)
    scale = 1.0 / math.sqrt(count)
    copies = []
    for j in range(share):
        values = []
        for a in range(count):
            block = blocks[where[a], j]
            values.append((block[0] * scale, block[1] * scale))
        for k, (re, im) in enumerate(butterfly(values)):
            out[k, j, 0] = re
            out[k, j, 1] = im
        copies.append(pltpu.make_async_copy(out.at[:, j], far.at[:, j], sem.at[j]))
        copies[-1].start()
    for copy in copies:
        copy.wait()


def split(x):
    high = x.astype(jnp.bfloat16)
    return high, (x - high.astype(jnp.float32)).astype(jnp.bfloat16)


def prepare_kernel(radial, high, low):
    high[...], low[...] = split(radial[...])


def invert_kernel(harm, r_high, r_low_far, far, x, r_low, out, sem):
    copy = pltpu.make_async_copy(r_low_far, r_low, sem.at[0])
    copy.start()
    cells, _, rows, lanes = harm.shape
    columns = r_high.shape[0]
    tiles = columns // lanes
    height = cells // tiles * rows
    for r in range(cells // tiles):
        for t in range(tiles):
            for c in range(2):
                high, low = split(harm[r * tiles + t, c])
                start = c * height + r * rows
                x[start : start + rows, t * lanes : t * lanes + lanes] = high
                x[2 * height + start : 2 * height + start + rows, t * lanes : t * lanes + lanes] = low
    span = columns // SPANS
    copies = []
    for i in range(SPANS):
        inside = slice(i * span, i * span + span)
        value = dot(x[...], r_high[:, inside])
        if i == 0:
            copy.wait()
        value = value[: 2 * height] + value[2 * height :] + dot(x[: 2 * height], r_low[:, inside])
        out[:, :, inside] = value.reshape(2, height, span)
        copies.append(pltpu.make_async_copy(out.at[:, :, inside], far.at[:, :, inside], sem.at[i + 1]))
        copies[-1].start()
    for copy in copies:
        copy.wait()


SPANS = 2
HBM = pltpu.MemorySpace.HBM


def call(kernel, out_shape, args, scratch=(), flops=0, scalars=0, far=(), limit=2, far_out=False):
    moved = sum(math.prod(x.shape) * x.dtype.itemsize for x in (*args, *jax.tree.leaves(out_shape)))
    specs = [SMEM] * scalars + [VMEM] * (len(args) - scalars)
    args = list(args)
    for i in far:
        args[i] = pltpu.with_memory_space_constraint(args[i], HBM)
        if i >= scalars:
            specs[i] = pl.BlockSpec(memory_space=HBM)
    return pl.pallas_call(
        kernel,
        out_shape=out_shape,
        in_specs=specs,
        out_specs=jax.tree.map(lambda _: pl.BlockSpec(memory_space=pl.ANY) if far_out else VMEM, out_shape),
        scratch_shapes=scratch,
        cost_estimate=pl.CostEstimate(flops=flops, bytes_accessed=moved, transcendentals=0),
        compiler_params=pltpu.CompilerParams(vmem_limit_bytes=limit << 20),
    )(*args)


def merge_kernel(*refs):
    total = refs[0][...]
    for x in refs[1:-1]:
        total = total + x[...]
    refs[-1][...] = total


def merge(parts):
    return call(merge_kernel, jax.ShapeDtypeStruct(parts[0].shape, parts[0].dtype), parts)


def all_sum(parts, axis, count):
    inner = len(parts)
    outer = count // inner

    def swap(x, mask):
        return lax.ppermute(x, axis, [(i, i ^ mask) for i in range(count)])

    others = [swap(parts[m], m) for m in range(1, inner)]
    total = merge([parts[0], *others])
    others = [swap(total, m * inner) for m in range(1, outer)]
    total = merge([total, *others])
    return [total] + [swap(total, m) for m in range(1, inner)]


def on_device(count, object_init, measured, positions, angle_list, probe, radial):
    f32, bf16 = jnp.float32, jnp.bfloat16
    shape = jax.ShapeDtypeStruct
    size = probe.shape[1]
    rows, columns = object_init.shape[2:]
    cells = rows // SUBLANES * (columns // LANES)
    patches = measured.shape[1]
    assert object_init.shape[0] == 1 and rows == size == LANES and cells % count == 0
    t1, t2 = transform_tables(size)
    obj, meas, pos = object_init[0], measured[0], positions[0].T
    flops = patches * 4 * 2 * (2 * size) * (2 * size) * size
    bits = count.bit_length() - 1
    inner, late = 1 << bits // 2, 1 << (bits + 2) // 2
    low = lax.axis_index("angle").reshape(1)
    messages = [shape((2 * size // inner + SUBLANES, LANES), f32)] * inner
    late_messages = [shape((2 * size // late + SUBLANES, LANES), f32)] * late
    field = shape((cells, 2, SUBLANES, LANES), f32)
    windows = (patches, 2, size, LANES)
    gradient = pltpu.VMEM((2 * size + SUBLANES, LANES), f32)
    obj, *parts = call(
        functools.partial(first_kernel, inner),
        [field, *messages],
        (low, pos, obj, meas, probe, t1, t2),
        [pltpu.VMEM(x.shape, x.dtype) for x in (obj, meas, probe, t1, t2)]
        + [pltpu.VMEM(windows, f32), gradient, pltpu.SemaphoreType.DMA((5,))],
        flops,
        2,
        far=range(1, 7),
        limit=16,
    )
    pieces, energy = call(
        cut_kernel, [shape(windows, f32), shape((SUBLANES, LANES), f32)], (pos, obj), (), 10 * obj.size, 1
    )
    r_high, r_low = call(prepare_kernel, [shape(radial.shape[1:], bf16)] * 2, (radial[0],), flops=3 * radial.size)
    blocks = all_sum(parts, "angle", count)
    prb, obj, *parts = call(
        functools.partial(second_kernel, inner),
        [shape(probe.shape, f32), field, *late_messages],
        (low, pos, obj, pieces, energy, meas, probe, t1, t2, *blocks),
        [gradient],
        flops,
        2,
        limit=16,
    )

    def exchange(x):
        return lax.all_to_all(x, "angle", split_axis=0, concat_axis=0, tiled=True)

    received = exchange(obj)
    grouped = shape((count, cells // count, 2, SUBLANES, LANES), f32)
    harm = call(
        angular_kernel,
        grouped,
        (angle_list, received.reshape(grouped.shape)),
        [
            pltpu.SMEM((count,), jnp.int32),
            pltpu.VMEM(grouped.shape, f32),
            pltpu.SemaphoreType.DMA((cells // count,)),
        ],
        10 * received.size,
        1,
        limit=8,
        far_out=True,
    ).reshape(field.shape)
    harm = exchange(harm)
    slices = call(
        invert_kernel,
        shape(object_init.shape[1:], f32),
        (harm, r_high, r_low),
        [
            pltpu.VMEM((4 * rows, columns), bf16),
            pltpu.VMEM(r_low.shape, bf16),
            pltpu.VMEM(object_init.shape[1:], f32),
            pltpu.SemaphoreType.DMA((SPANS + 1,)),
        ],
        6 * 2 * rows * columns * columns,
        0,
        far=(2,),
        limit=12,
        far_out=True,
    )
    blocks = all_sum(parts, "angle", count)
    probe_out = call(probe_kernel, shape(probe.shape, f32), (low, prb, *blocks), scalars=1)
    return slices[None], probe_out


def solution(mesh):
    count = mesh.shape["angle"]

    def body(*args):
        return on_device(count, *args)

    in_specs = (
        P(("scan", "angle"), None, None, None),
        P(("scan", "angle"), None, None, None),
        P(("scan", "angle"), None, None),
        P("scan"),
        P("scan", None, None),
        P("angle", None, None),
    )
    out_specs = (P(("scan", "angle"), None, None, None), P("scan", None, None))
    return jax.shard_map(body, mesh=mesh, in_specs=in_specs, out_specs=out_specs, check_vma=False)
```

```python
import functools
import math

import jax
import jax.numpy as jnp
import numpy as np
from jax import lax
from jax.experimental import pallas as pl
from jax.experimental.pallas import tpu as pltpu
from jax.sharding import PartitionSpec as P


LANES = 128
SUBLANES = 8

object_rate = 0.5
probe_rate = 1.0

VMEM = pl.BlockSpec(memory_space=pltpu.VMEM)
SMEM = pl.BlockSpec(memory_space=pltpu.SMEM)


def transform_tables(size):
    index = np.arange(size, dtype=np.int32)
    phase = index[:, None] * index[None, :] % size
    angle = phase.astype(np.float32) * np.float32(2.0 * math.pi / size)
    scale = np.float32(1.0 / math.sqrt(size))
    c = (np.cos(angle) * scale).astype(jnp.bfloat16)
    s = (np.sin(angle) * scale).astype(jnp.bfloat16)
    t = np.block([[c, s], [-s, c]])
    return jnp.asarray(t), jnp.asarray(np.ascontiguousarray(t.T))


def dot(a, b):
    return jnp.dot(a, b, preferred_element_type=jnp.float32)


def window(pos, n, tiles):
    col = pos[1, n]
    q = jnp.minimum(col // LANES, tiles - 2)
    rem = col - q * LANES
    return q, rem


def cut(load, q, rem, mask):
    y = jnp.where(mask, load(q), load(q + 1))
    return pltpu.roll(y, lax.rem(LANES - rem, LANES), 1)


def iterate(pos, piece, measured, probe, t1, t2, out, pg, placed=None):
    size = probe.shape[1]
    patches = measured.shape[0]
    tiles = out.shape[0] // (size // SUBLANES)
    view = out.reshape(size // SUBLANES, tiles, 2, SUBLANES, LANES)
    lane = lax.broadcasted_iota(jnp.int32, (size, LANES), 1)
    prb_re, prb_im = probe[0], probe[1]
    rate = object_rate / jnp.max(prb_re * prb_re + prb_im * prb_im)

    def both(a, b):
        return jnp.concatenate([a.astype(jnp.bfloat16), b.astype(jnp.bfloat16)], 0)

    def regroup(x):
        x = x.astype(jnp.bfloat16)
        spans = [slice(i * size, (i + 1) * size) for i in range(patches)]
        return jnp.concatenate([jnp.concatenate([x[:size, p], x[size:, p]], 1) for p in spans], 0)

    waves = []
    for n in range(patches):
        a, b = piece(n)
        waves.append(both(prb_re * a - prb_im * b, prb_re * b + prb_im * a))
    half = regroup(dot(t1[...], jnp.concatenate(waves, 1)))
    far = dot(half, t2[...])
    pushes = []
    for n in range(patches):
        rows = slice(n * size, (n + 1) * size)
        fr, fi = far[rows, :size], far[rows, size:]
        resid = fr * fr + fi * fi - measured[n].astype(jnp.float32)
        pushes.append(both(resid * fr, resid * fi))
    back = regroup(dot(t2[...], jnp.concatenate(pushes, 1)))
    grad = dot(back, t1[...])
    total_re = total_im = 0.0
    step_re, step_im = prb_re * rate, prb_im * rate
    for n in range(patches):
        rows = slice(n * size, (n + 1) * size)
        gr, gi = grad[rows, :size], grad[rows, size:]
        a, b = piece(n)
        total_re, total_im = total_re + (a * gr + b * gi), total_im + (a * gi - b * gr)
        q, rem = window(pos, n, tiles)
        mask = lane >= rem
        for c, value in ((0, step_re * gr + step_im * gi), (1, step_re * gi - step_im * gr)):
            r = pltpu.roll(value, lax.rem(rem, LANES), 1)
            r = r.reshape(size // SUBLANES, SUBLANES, LANES)
            for t, own in ((q, mask), (q + 1, ~mask)):
                pltpu.store(view.at[:, t, c], view[:, t, c] - r, mask=own.reshape(r.shape))
        if placed:
            placed(n, view)
    pg[:size] = total_re
    pg[size : 2 * size] = total_im


def energy_of(piece, patches):
    total = 0.0
    for n in range(patches):
        for x in piece(n):
            total = total + (x * x).reshape(-1, SUBLANES, LANES).sum(0)
    return total


def hand_out(low, pg, parts):
    if len(parts) == 2:
        height = (parts[0].shape[0] - SUBLANES) // 2
        for m, part in enumerate(parts):
            for i in range(2):
                start = pl.multiple_of((low[0] & 3 ^ (m + 2 * i)) * height, SUBLANES)
                part[i * height : i * height + height] = pg[pl.ds(start, height)]
            part[2 * height :] = pg[4 * height :]
        return
    height = parts[0].shape[0] - SUBLANES
    for m, part in enumerate(parts):
        start = pl.multiple_of((low[0] & (len(parts) - 1) ^ m) * height, SUBLANES)
        part[:height] = pg[pl.ds(start, height)]
        part[height:] = pg[height * len(parts) :]


def collect(low, blocks, probe, out):
    height = blocks[0].shape[0] - SUBLANES
    size = probe.shape[1]
    energy = jnp.sum(blocks[0][height:]) / (size * size)
    share = min(height, size)
    for m, block in enumerate(blocks):
        for piece in range(height // share):
            start = (low[0] & (len(blocks) - 1) ^ m) * height + piece * share
            where = (start // size, pl.ds(pl.multiple_of(start % size, SUBLANES), share))
            gradient = block[piece * share : piece * share + share]
            out[where] = probe[where] - probe_rate * gradient / energy


def first_kernel(handed, low, pos, obj_far, measured_far, probe_far, t1_far, t2_far, out, *refs):
    parts, (obj, measured, probe, t1, t2, pieces, pg, sem) = refs[:handed], refs[handed:]
    pairs = ((probe_far, probe), (obj_far, obj), (t1_far, t1), (t2_far, t2), (measured_far, measured))
    copies = [pltpu.make_async_copy(far, near, sem.at[i]) for i, (far, near) in enumerate(pairs)]
    for copy in copies:
        copy.start()
    size = probe.shape[1]
    patches, tiles = measured.shape[0], obj.shape[2] // LANES
    lane = lax.broadcasted_iota(jnp.int32, (size, LANES), 1)
    copies[0].wait()
    copies[1].wait()
    for n in range(patches):
        q, rem = window(pos, n, tiles)
        mask = lane >= rem
        for c in range(2):

            def load(t):
                return obj[c, :, pl.ds(pl.multiple_of(t * LANES, LANES), LANES)]

            pieces[n, c] = cut(load, q, rem, mask)
    for r in range(size // SUBLANES):
        for t in range(tiles):
            for c in range(2):
                out[r * tiles + t, c] = obj[c, r * 8 : r * 8 + 8, t * 128 : t * 128 + 128]

    def piece(n):
        return pieces[n, 0], pieces[n, 1]

    pg[2 * size :] = energy_of(piece, patches)
    for copy in copies[2:]:
        copy.wait()
    iterate(pos, piece, measured, probe, t1, t2, out, pg)
    hand_out(low, pg, parts)


def cut_kernel(pos, obj, pieces, energy):
    patches, _, size, _ = pieces.shape
    tiles = obj.shape[0] // (size // SUBLANES)
    view = obj.reshape(size // SUBLANES, tiles, 2, SUBLANES, LANES)
    lane = lax.broadcasted_iota(jnp.int32, (size, LANES), 1)
    energy[...] = jnp.zeros_like(energy)

    def body(n, carry):
        q, rem = window(pos, n, tiles)
        mask = lane >= rem
        for c in range(2):
            x = cut(lambda t: view[:, t, c].reshape(size, LANES), q, rem, mask)
            pieces[n, c] = x
            energy[...] += (x * x).reshape(-1, SUBLANES, LANES).sum(0)
        return carry

    lax.fori_loop(0, patches, body, 0)


def second_kernel(inner, low, pos, obj, pieces, energy, measured, probe, t1, t2, *refs):
    blocks, prb_out, far, refs = refs[:inner], refs[inner], refs[inner + 1], refs[inner + 2 :]
    parts, (out, staged, pg, sem) = refs[:-4], refs[-4:]
    tiles = out.shape[0] // (probe.shape[1] // SUBLANES)
    far = far.reshape(out.shape[0] // tiles, tiles, 2, SUBLANES, LANES)
    copies = []

    def placed(n, view):
        ready = tiles if n + 1 == measured.shape[0] else n // 2
        for t in range(len(copies), ready):
            staged[:, t] = view[:, t]
            copies.append(pltpu.make_async_copy(staged.at[:, t], far.at[:, t], sem.at[t]))
            copies[-1].start()

    size = probe.shape[1]
    collect(low, blocks, probe, prb_out)
    pg[2 * size :] = energy[...]
    out[...] = obj[...]
    iterate(pos, lambda n: (pieces[n, 0], pieces[n, 1]), measured, prb_out, t1, t2, out, pg, placed)
    hand_out(low, pg, parts)
    for copy in copies:
        copy.wait()


def probe_kernel(low, probe, *refs):
    collect(low, refs[:-1], probe, refs[-1])


def butterfly(values):
    n = len(values)
    if n == 1:
        return values
    even, odd = butterfly(values[::2]), butterfly(values[1::2])
    low, high = [], []
    for k in range(n // 2):
        (er, ei), (xr, xi) = even[k], odd[k]
        c, s = math.cos(2 * math.pi * k / n), -math.sin(2 * math.pi * k / n)
        if k == 0:
            tr, ti = xr, xi
        elif 4 * k == n:
            tr, ti = xi, -xr
        elif 8 * k == n:
            tr, ti = (xr + xi) * c, (xi - xr) * c
        elif 8 * k == 3 * n:
            tr, ti = (xr * c - xi * s), (xr * s + xi * c)
        else:
            tr, ti = xr * c - xi * s, xr * s + xi * c
        low.append((er + tr, ei + ti))
        high.append((er - tr, ei - ti))
    return low + high


def angular_kernel(angles, blocks, far, where, out, sem):
    count, share = blocks.shape[:2]

    def note(b, carry):
        where[angles[b]] = b
        return carry

    lax.fori_loop(0, count, note, 0)
    scale = 1.0 / math.sqrt(count)
    copies = []
    for j in range(share):
        values = []
        for a in range(count):
            block = blocks[where[a], j]
            values.append((block[0] * scale, block[1] * scale))
        for k, (re, im) in enumerate(butterfly(values)):
            out[k, j, 0] = re
            out[k, j, 1] = im
        copies.append(pltpu.make_async_copy(out.at[:, j], far.at[:, j], sem.at[j]))
        copies[-1].start()
    for copy in copies:
        copy.wait()


def split(x):
    high = x.astype(jnp.bfloat16)
    return high, (x - high.astype(jnp.float32)).astype(jnp.bfloat16)


def prepare_kernel(radial, high, low):
    high[...], low[...] = split(radial[...])


def invert_kernel(harm, r_high, r_low_far, far, x, r_low, out, sem):
    height = r_low.shape[0] // PIECES
    shares = [slice(i * height, i * height + height) for i in range(PIECES)]
    loads = [pltpu.make_async_copy(r_low_far.at[p], r_low.at[p], sem.at[i]) for i, p in enumerate(shares)]
    for copy in loads:
        copy.start()
    cells, _, rows, lanes = harm.shape
    columns = r_high.shape[0]
    tiles = columns // lanes
    height = cells // tiles * rows
    for r in range(cells // tiles):
        for t in range(tiles):
            for c in range(2):
                high, low = split(harm[r * tiles + t, c])
                start = c * height + r * rows
                x[start : start + rows, t * lanes : t * lanes + lanes] = high
                x[2 * height + start : 2 * height + start + rows, t * lanes : t * lanes + lanes] = low
    span = columns // SPANS
    spans = [slice(i * span, i * span + span) for i in range(SPANS)]
    sums = []
    for inside in spans:
        value = dot(x[...], r_high[:, inside])
        sums.append(value[: 2 * height] + value[2 * height :])
    for copy in loads:
        copy.wait()
    copies = []
    for i, inside in enumerate(spans):
        value = sums[i] + dot(x[: 2 * height], r_low[:, inside])
        out[:, :, inside] = value.reshape(2, height, span)
        copies.append(pltpu.make_async_copy(out.at[:, :, inside], far.at[:, :, inside], sem.at[PIECES + i]))
        copies[-1].start()
    for copy in copies:
        copy.wait()


PIECES = 8
SPANS = 4
HBM = pltpu.MemorySpace.HBM


def call(kernel, out_shape, args, scratch=(), flops=0, scalars=0, far=(), limit=2, far_out=()):
    moved = sum(math.prod(x.shape) * x.dtype.itemsize for x in (*args, *jax.tree.leaves(out_shape)))
    specs = [SMEM] * scalars + [VMEM] * (len(args) - scalars)
    args = list(args)
    for i in far:
        args[i] = pltpu.with_memory_space_constraint(args[i], HBM)
        if i >= scalars:
            specs[i] = pl.BlockSpec(memory_space=HBM)

    def place(i):
        return pl.BlockSpec(memory_space=pl.ANY) if i in far_out else VMEM

    return pl.pallas_call(
        kernel,
        out_shape=out_shape,
        in_specs=specs,
        out_specs=[place(i) for i in range(len(out_shape))] if isinstance(out_shape, list) else place(0),
        scratch_shapes=scratch,
        cost_estimate=pl.CostEstimate(flops=flops, bytes_accessed=moved, transcendentals=0),
        compiler_params=pltpu.CompilerParams(vmem_limit_bytes=limit << 20),
    )(*args)


def merge_kernel(*refs):
    total = refs[0][...]
    for x in refs[1:-1]:
        total = total + x[...]
    refs[-1][...] = total


def merge(parts):
    return call(merge_kernel, jax.ShapeDtypeStruct(parts[0].shape, parts[0].dtype), parts)


def halve_kernel(kept, got, *outs):
    for i, out in enumerate(outs):
        height = out.shape[0] - SUBLANES
        for rows, source in ((slice(0, height), slice(i * height, i * height + height)),
                             (slice(height, height + SUBLANES), slice(len(outs) * height, len(outs) * height + SUBLANES))):
            out[rows] = kept[source] + got[source]


def all_sum(parts, axis, count):
    inner = len(parts)
    outer = count // inner

    def swap(x, mask):
        return lax.ppermute(x, axis, [(i, i ^ mask) for i in range(count)])

    if len(parts) == 2:
        inner = 4
        outer = count // inner
        got = swap(parts[1], 1)
        height = (parts[0].shape[0] - SUBLANES) // 2 + SUBLANES
        kept, sent = call(halve_kernel, [jax.ShapeDtypeStruct((height, LANES), jnp.float32)] * 2, (parts[0], got))
        got = swap(sent, 2)
        total = merge([kept, got])
    else:
        others = [swap(parts[m], m) for m in range(1, inner)]
        total = merge([parts[0], *others])
    others = [swap(total, m * inner) for m in range(1, outer)]
    total = merge([total, *others])
    return [total] + [swap(total, m) for m in range(1, inner)]


def on_device(count, object_init, measured, positions, angle_list, probe, radial):
    f32, bf16 = jnp.float32, jnp.bfloat16
    shape = jax.ShapeDtypeStruct
    size = probe.shape[1]
    rows, columns = object_init.shape[2:]
    cells = rows // SUBLANES * (columns // LANES)
    patches = measured.shape[1]
    assert object_init.shape[0] == 1 and rows == size == LANES and cells % count == 0
    t1, t2 = transform_tables(size)
    obj, meas, pos = object_init[0], measured[0], positions[0].T
    flops = patches * 4 * 2 * (2 * size) * (2 * size) * size
    bits = count.bit_length() - 1
    inner, late = 1 << bits // 2, 1 << (bits + 2) // 2
    low = lax.axis_index("angle").reshape(1)
    late_messages = [shape((2 * size // late + SUBLANES, LANES), f32)] * late
    field = shape((cells, 2, SUBLANES, LANES), f32)
    windows = (patches, 2, size, LANES)
    gradient = pltpu.VMEM((2 * size + SUBLANES, LANES), f32)
    handed = inner
    early = [shape((2 * size // handed + SUBLANES, LANES), f32)] * handed
    obj, *parts = call(
        functools.partial(first_kernel, handed),
        [field, *early],
        (low, pos, obj, meas, probe, t1, t2),
        [pltpu.VMEM(x.shape, x.dtype) for x in (obj, meas, probe, t1, t2)]
        + [pltpu.VMEM(windows, f32), gradient, pltpu.SemaphoreType.DMA((5,))],
        flops,
        2,
        far=range(1, 7),
        limit=16,
    )
    pieces, energy = call(
        cut_kernel, [shape(windows, f32), shape((SUBLANES, LANES), f32)], (pos, obj), (), 10 * obj.size, 1
    )
    r_high, r_low = call(prepare_kernel, [shape(radial.shape[1:], bf16)] * 2, (radial[0],), flops=3 * radial.size)
    blocks = all_sum(parts, "angle", count)
    prb, obj, *parts = call(
        functools.partial(second_kernel, inner),
        [shape(probe.shape, f32), field, *late_messages],
        (low, pos, obj, pieces, energy, meas, probe, t1, t2, *blocks),
        [
            pltpu.VMEM(field.shape, f32),
            pltpu.VMEM((rows // SUBLANES, columns // LANES, 2, SUBLANES, LANES), f32),
            gradient,
            pltpu.SemaphoreType.DMA((columns // LANES,)),
        ],
        flops,
        2,
        limit=16,
        far_out=(1,),
    )

    def exchange(x):
        return lax.all_to_all(x, "angle", split_axis=0, concat_axis=0, tiled=True)

    received = exchange(obj)
    grouped = shape((count, cells // count, 2, SUBLANES, LANES), f32)
    harm = call(
        angular_kernel,
        grouped,
        (angle_list, received.reshape(grouped.shape)),
        [
            pltpu.SMEM((count,), jnp.int32),
            pltpu.VMEM(grouped.shape, f32),
            pltpu.SemaphoreType.DMA((cells // count,)),
        ],
        10 * received.size,
        1,
        limit=8,
        far_out=(0,),
    ).reshape(field.shape)
    harm = exchange(harm)
    slices = call(
        invert_kernel,
        shape(object_init.shape[1:], f32),
        (harm, r_high, r_low),
        [
            pltpu.VMEM((4 * rows, columns), bf16),
            pltpu.VMEM(r_low.shape, bf16),
            pltpu.VMEM(object_init.shape[1:], f32),
            pltpu.SemaphoreType.DMA((PIECES + SPANS,)),
        ],
        6 * 2 * rows * columns * columns,
        0,
        far=(2,),
        limit=12,
        far_out=(0,),
    )
    blocks = all_sum(parts, "angle", count)
    probe_out = call(probe_kernel, shape(probe.shape, f32), (low, prb, *blocks), scalars=1)
    return slices[None], probe_out


def solution(mesh):
    count = mesh.shape["angle"]

    def body(*args):
        return on_device(count, *args)

    in_specs = (
        P(("scan", "angle"), None, None, None),
        P(("scan", "angle"), None, None, None),
        P(("scan", "angle"), None, None),
        P("scan"),
        P("scan", None, None),
        P("angle", None, None),
    )
    out_specs = (P(("scan", "angle"), None, None, None), P("scan", None, None))
    return jax.shard_map(body, mesh=mesh, in_specs=in_specs, out_specs=out_specs, check_vma=False)
```
